128 devices in a mesh: rep: 4 (over z_lo, core), row: 8 (over z_hi, y), col: 4 (over x).
Axes of the slice: x: 4, y: 4, z: 4 (z_hi: 2, z_lo: 2; z = z_hi * 2 + z_lo), core: 2. Of those that a mesh axis runs over, the one named last changes fastest.
Arguments:
- activations: bfloat16 [4096, 8192], P(('rep', 'row'), 'col'), may hold values from -12 to 12
- target: bfloat16 [4096, 8192], P(('rep', 'col'), 'row'), may hold values from -6 to 6
- weight: bfloat16 [8192, 8192], P('col', 'row'), may hold values from -0.0625 to 0.0625
- probe_codes: int32 [4, 8], P('col', 'row'), may hold values from 0 to 1073741823
Outputs:
- step: bfloat16 [8192, 8192], P('col', 'row')
The draws below stay inside these ranges and needn't reach their ends.
All inputs are finite; a program needn't handle non-finite values.
Results may differ from the reference program's by a relative error of at most 0.018.
Values may be sent and summed in bfloat16 or wider, within the bound.
A program may use at most 128 MiB of HBM per device.

```python
import math
import jax
import jax.numpy as jnp

D = 8192
TOK = 1024
AVG = 128
TOKENS = 4096
N_REP = 4
N_ROW = 8
N_COL = 4


def draw_activations(key, part):
    feature_key = jax.random.fold_in(key, 11)
    value_key = jax.random.fold_in(key, 12)
    feature_scale = jnp.exp(jax.random.uniform(feature_key, (1, D), jnp.float32, jnp.log(0.3), jnp.log(3.0)))
    values = jax.random.truncated_normal(value_key, -4.0, 4.0, (TOKENS, D), jnp.float32)
    whole = values * feature_scale
    return jnp.clip(whole, -12.0, 12.0).astype(jnp.bfloat16)


def set_ends(result, own_key, smallest, top_value):
    index_at = [jax.random.randint(jax.random.fold_in(own_key, axis), (), 0, length) for axis, length in enumerate(result.shape)]
    main_axis = result.shape.index(max(result.shape))
    neighbour = index_at[:main_axis] + [(index_at[main_axis] + 1) % result.shape[main_axis]] + index_at[main_axis + 1:]
    return result.at[tuple(index_at)].set(smallest).at[tuple(neighbour)].set(top_value)


def levels(own_key, shape, cuts, low, high):
    loudness = 1.0
    for position, blocks in cuts:
        draws = jax.random.uniform(jax.random.fold_in(jax.random.fold_in(own_key, 6), position), (blocks,), jnp.float32, low / len(cuts), high / len(cuts))
        loudness = loudness * jnp.repeat(jnp.exp(draws), shape[position] // blocks).reshape((-1,) + (1,) * (len(shape) - 1 - position))
    return loudness


def normal_values(own_key, shape, scale, most, shards=(), kind=jnp.bfloat16):
    array = scale * jax.random.normal(own_key, shape, jnp.float32)
    if shards:
        array = array * levels(own_key, shape, shards, -0.22, 0.18)
    return jnp.clip(array, -most, most).astype(kind)


def setup_inputs(seed: int = 0) -> dict:
    arg_keys = jax.random.split(jax.random.key(seed), 5)
    activations = draw_activations(jax.random.fold_in(arg_keys[4], 71), 0)
    target = normal_values(arg_keys[1], (TOKENS, D), 1.0, 6.0, ((0, 16), (1, 8)))
    weight = normal_values(arg_keys[2], (D, D), D ** -0.5, 0.0625, ((0, 4), (1, 8)))
    probe_codes = set_ends(jax.random.randint(arg_keys[3], (N_COL, N_ROW), 0, 1073741824), jax.random.fold_in(arg_keys[3], 1), 0, 1073741823).astype(jnp.int32)
    return dict(activations=activations, target=target, weight=weight, probe_codes=probe_codes)


def probe_signs(tile_code, local_rows, local_cols):
    mixed = local_rows * 1664525 + local_cols * 22695477 + tile_code * 1013904223
    mixed = mixed ^ mixed >> 15 & 131071
    mixed = mixed * 1274126177
    mixed = mixed ^ mixed >> 13 & 524287
    parity = mixed >> 7 & 1
    return (1 - 2 * parity).astype(jnp.float32).astype(jnp.bfloat16)

def finish(gradient, curvature):
    rows, cols = curvature.shape
    blockmean = curvature.reshape(rows, cols // AVG, AVG).mean(axis=2, keepdims=True)
    denom = jnp.maximum(jnp.abs(blockmean), 0.25)
    update = gradient.reshape(rows, cols // AVG, AVG) / denom
    return update.reshape(rows, cols).astype(jnp.bfloat16)

def reference(activations, target, weight, probe_codes):
    rows_tile = D // N_COL
    cols_tile = D // N_ROW
    index = jnp.arange(D, dtype=jnp.int32)
    tile_codes = probe_codes[(index // rows_tile)[:, None], (index // cols_tile)[None, :]]
    probe = probe_signs(tile_codes, (index % rows_tile)[:, None], (index % cols_tile)[None, :])
    grad_scale = 1.0 / math.sqrt(TOKENS)
    curv_scale = 1.0 / TOKENS
    gradient = jnp.zeros((D, D), jnp.float32)
    curvature = jnp.zeros((D, D), jnp.float32)
    for micro in range(N_REP):
        block = activations[micro * TOK:(micro + 1) * TOK]
        wanted = target[micro * TOK:(micro + 1) * TOK]
        output = jnp.dot(block, weight, preferred_element_type=jnp.float32)
        error = (output - wanted.astype(jnp.float32)).astype(jnp.bfloat16)
        tangent = jnp.dot(block, probe, preferred_element_type=jnp.float32).astype(jnp.bfloat16)
        grad_part = (jnp.dot(block.T, error, preferred_element_type=jnp.float32) * grad_scale).astype(jnp.bfloat16)
        curv_part = probe.astype(jnp.float32) * jnp.dot(block.T, tangent, preferred_element_type=jnp.float32) * curv_scale
        gradient = gradient + grad_part.astype(jnp.float32)
        curvature = curvature + curv_part
    return finish(gradient, curvature)
```

```python
import functools
import math

import jax
import jax.numpy as jnp
from jax import lax
from jax.experimental import pallas as pl
from jax.experimental.pallas import tpu as pltpu
from jax.sharding import PartitionSpec as P

MESH = pl.DeviceIdType.MESH
BF = jnp.bfloat16
F32 = jnp.float32
AVG = 128
SUB = 16
GROUPS = ((0, 1, None), (1, 4, 0), (1, 4, 1), (4, 5, None), (5, 8, 0), (5, 8, 1))


def wrapped(value):
    return (value + 2**31) % 2**32 - 2**31


def remote(src, dst, send, recv, peer):
    return pltpu.make_async_remote_copy(
        src_ref=src, dst_ref=dst, send_sem=send, recv_sem=recv,
        device_id=peer, device_id_type=MESH,
    )


def kernel(
    grad_scale, curv_scale, code_ref, x_hbm, y_hbm, w_hbm, out_hbm,
    xg, w, y, pt, own, hold_e, hold_t, sb_p, sb_m, s2_p, s2_m, rb_p, rb_m, r2_p, r2_m,
    et, g_own, m_own, g_send, m_send, g_recv, m_recv, h_send, n_send, h_recv, n_recv, stage,
    load_sem, xs, xr, rs_s, rs_r, ag_s, ag_r, co_s, co_r, zs, zr, fs, fr, ls,
):
    rep, row, col = lax.axis_index("rep"), lax.axis_index("row"), lax.axis_index("col")
    plane, ypos = row // 4, row % 4
    core = rep % 2
    right, left, far = (col + 1) % 4, (col + 3) % 4, (col + 2) % 4
    to_right, to_left = {"col": right}, {"col": left}
    up, down = {"row": plane * 4 + (ypos + 1) % 4}, {"row": plane * 4 + (ypos + 3) % 4}
    across = {"row": (row + 4) % 8}
    twin = {"rep": rep - core + (1 - core)}
    zmate = {"rep": (rep + 2) % 4}
    rows, cols = w.shape
    nc = cols // AVG
    half = rows // 2

    loads = [
        pltpu.make_async_copy(x_hbm, xg.at[:, 0], load_sem.at[0]),
        pltpu.make_async_copy(w_hbm, w, load_sem.at[1]),
        pltpu.make_async_copy(y_hbm, y, load_sem.at[2]),
    ]
    for load in loads:
        load.start()

    barrier = pltpu.get_barrier_semaphore()
    peers = (to_right, to_left, up, down, across, twin, zmate)
    for peer in peers:
        pl.semaphore_signal(barrier, inc=1, device_id=peer, device_id_type=MESH)
    pl.semaphore_wait(barrier, len(peers))
    loads[0].wait()

    sent = []

    def pass_on(slot, part, peer, landing):
        k = len(sent)
        copy = remote(xg.at[:, slot, part], xg.at[:, landing, part], xs.at[k], xr.at[landing, part], peer)
        copy.start()
        sent.append(copy)

    def arrived(slot, part):
        remote(xg.at[:, slot, part], xg.at[:, slot, part], xs.at[0], xr.at[slot, part], across).wait_recv()

    for part in range(2):
        pass_on(0, part, across, 1)
        pass_on(0, part, up, 3)
        pass_on(0, part, down, 2)

    loads[1].wait()
    loads[2].wait()

    slot_rows = []
    other = 1 - plane
    for pl_, dy in ((plane, 0), (other, 0), (plane, 1), (plane, 3), (plane, 2), (other, 1), (other, 3), (other, 2)):
        slot_rows.append(pl_ * 4 + (ypos + dy) % 4)

    def units(group):
        lo, hi, part = GROUPS[group]
        return [(s, h) for s in range(lo, hi) for h in ((0, 1) if part is None else (part,))]

    def view(ref, group, lanes=slice(None)):
        lo, hi, part = GROUPS[group]
        return ref.at[lo:hi, :, :, lanes] if part is None else ref.at[lo:hi, part, :, lanes]

    def members(group):
        lo, hi, part = GROUPS[group]
        n = len(units(group))
        pieces = []
        for k in range(4):
            dest = (col + k) % 4
            piece = xg[dest, lo:hi] if part is None else xg[dest, lo:hi, part]
            pieces.append(piece.reshape(n * SUB, rows))
        return jnp.concatenate(pieces, axis=0)

    def put(ref, group, lanes, value):
        lo, hi, part = GROUPS[group]
        if part is None:
            ref[lo:hi, :, :, lanes] = value.reshape(hi - lo, 2, SUB, value.shape[-1])
        else:
            ref[lo:hi, part, :, lanes] = value.reshape(hi - lo, SUB, value.shape[-1])

    def get(ref, group, lanes):
        lo, hi, part = GROUPS[group]
        value = ref[lo:hi, :, :, lanes] if part is None else ref[lo:hi, part, :, lanes]
        return value.reshape(len(units(group)) * SUB, value.shape[-1])

    BLOCK = 256

    def errors(group):
        n = len(units(group)) * SUB

        def step(j, carry):
            lanes = pl.ds(pl.multiple_of(j * BLOCK, BLOCK), BLOCK)
            sums = jnp.dot(members(group), w[:, lanes], preferred_element_type=F32)
            parts = []
            for k in range(4):
                dest = (col + k) % 4
                wanted = []
                for s, h in units(group):
                    mine = (slot_rows[s] // 2 == col).astype(F32)
                    wanted.append(y[slot_rows[s] % 2, dest, h, :, lanes].astype(F32) * mine)
                parts.append(sums[k * n:(k + 1) * n] - jnp.concatenate(wanted, axis=0))
            put(own, group, lanes, parts[0])
            put(hold_e, group, lanes, parts[1])
            put(sb_p, group, lanes, parts[2].astype(BF))
            put(sb_m, group, lanes, parts[3].astype(BF))
            return carry

        lax.fori_loop(0, cols // BLOCK, step, 0)

    def tangents(group):
        n = len(units(group)) * SUB

        def step(j, carry):
            start = pl.multiple_of(j * BLOCK, BLOCK)
            lanes, shifted = pl.ds(start, BLOCK), pl.ds(pl.multiple_of(cols + start, BLOCK), BLOCK)
            sums = lax.dot_general(
                members(group), pt[lanes, :], (((1,), (1,)), ((), ())), preferred_element_type=F32
            )
            parts = [sums[k * n:(k + 1) * n] for k in range(4)]
            put(own, group, shifted, parts[0])
            put(sb_p, group, shifted, parts[1].astype(BF))
            put(sb_m, group, shifted, parts[2].astype(BF))
            put(hold_t, group, lanes, parts[3])
            return carry

        lax.fori_loop(0, cols // BLOCK, step, 0)

    def first_hop(group):
        return [
            remote(view(sb_p, group), view(rb_p, group), rs_s.at[0, group], rs_r.at[0, group], to_right),
            remote(view(sb_m, group), view(rb_m, group), rs_s.at[1, group], rs_r.at[1, group], to_left),
        ]

    def second_hop(group):
        return [
            remote(view(s2_p, group), view(r2_p, group), rs_s.at[2, group], rs_r.at[2, group], to_right),
            remote(view(s2_m, group), view(r2_m, group), rs_s.at[3, group], rs_r.at[3, group], to_left),
        ]

    def relay(group):
        for copy in first_hop(group):
            copy.wait_recv()
        low, high = slice(0, cols), slice(cols, 2 * cols)
        put(s2_p, group, low, (get(hold_e, group, low) + get(rb_p, group, low).astype(F32)).astype(BF))
        put(s2_m, group, low, (get(hold_t, group, low) + get(rb_m, group, high).astype(F32)).astype(BF))
        for copy in second_hop(group):
            copy.start()

    def probe_signs():
        code = code_ref[0, 0] * 1013904223
        lane = lax.broadcasted_iota(jnp.int32, (SUB, 512), 1) * 1664525
        sub = lax.broadcasted_iota(jnp.int32, (SUB, 512), 0) * 22695477
        base = lane + sub + code

        def step(j, carry):
            for i in range(rows // 512):
                mixed = base + (j * (SUB * 22695477) + wrapped(i * 512 * 1664525))
                mixed = mixed ^ mixed >> 15 & 131071
                mixed = mixed * 1274126177
                mixed = mixed ^ mixed >> 13 & 524287
                parity = mixed >> 7 & 1
                pt[pl.ds(pl.multiple_of(j * SUB, SUB), SUB), i * 512:(i + 1) * 512] = (
                    (1 - 2 * parity).astype(F32).astype(BF)
                )
            return carry

        lax.fori_loop(0, cols // SUB, step, 0)

    errors(0)
    probe_signs()
    tangents(0)
    for copy in first_hop(0):
        copy.start()

    def forward_first():
        for s in (1, 2, 3):
            arrived(s, 0)
        pass_on(3, 0, up, 4)
        pass_on(1, 0, up, 6)
        pass_on(1, 0, down, 5)

    def forward_second():
        for s in (1, 2, 3):
            arrived(s, 1)
        pass_on(2, 1, down, 4)
        pass_on(1, 1, up, 6)
        pass_on(1, 1, down, 5)

    def forward_third():
        for part in range(2):
            arrived(4, part)
            pass_on(4, part, across, 7)

    def last(part):
        for s in (5, 6, 7):
            arrived(s, part)

    ready = (None, forward_first, forward_second, forward_third, lambda: last(0), lambda: last(1))
    for group in range(1, len(GROUPS)):
        ready[group]()
        errors(group)
        tangents(group)
        for copy in first_hop(group):
            copy.start()
        relay(group - 1)
    relay(len(GROUPS) - 1)
    for group in range(len(GROUPS)):
        for copy in second_hop(group):
            copy.wait_recv()

    def own_block(c):
        return [
            remote(et.at[c, col], et.at[c, col], ag_s.at[0, c], ag_r.at[0, c], to_right),
            remote(et.at[c, col], et.at[c, col], ag_s.at[1, c], ag_r.at[1, c], to_left),
        ]

    def far_block(c):
        first, second = slice(0, AVG), slice(AVG, 2 * AVG)
        return [
            remote(et.at[c, left, first], et.at[c, left, first], ag_s.at[2, c], ag_r.at[2, c], to_right),
            remote(et.at[c, right, second], et.at[c, right, second], ag_s.at[3, c], ag_r.at[3, c], to_left),
        ]

    def twin_block(c):
        return [
            remote(g_send.at[c], g_recv.at[c], co_s.at[0, c], co_r.at[0, c], twin),
            remote(m_send.at[c], m_recv.at[c], co_s.at[1, c], co_r.at[1, c], twin),
        ]

    def z_block(c):
        return [
            remote(h_send.at[c], h_recv.at[c], zs.at[0, c], zr.at[0, c], zmate),
            remote(n_send.at[c], n_recv.at[c], zs.at[1, c], zr.at[1, c], zmate),
        ]

    def result(c):
        area = out_hbm.at[
            pl.ds(pl.multiple_of(core * half, half), half), pl.ds(pl.multiple_of(c * AVG, AVG), AVG)
        ]
        return remote(stage.at[c], area, fs.at[c], fr.at[c], twin), pltpu.make_async_copy(
            stage.at[c], area, ls.at[c]
        )

    tokens = own.shape[0] * own.shape[1] * SUB

    def share(c):
        low = pl.ds(pl.multiple_of(c * AVG, AVG), AVG)
        high = pl.ds(pl.multiple_of(cols + c * AVG, AVG), AVG)

        def all_of(ref, lanes):
            return ref[:, :, :, lanes].reshape(tokens, AVG).astype(F32)

        error = all_of(own, low) + all_of(rb_m, low) + all_of(r2_p, low)
        tangent = all_of(own, high) + all_of(rb_p, high) + all_of(r2_m, low)
        et[c, col, 0:AVG] = error.T.astype(BF)
        et[c, col, AVG:2 * AVG] = tangent.T.astype(BF)
        for copy in own_block(c):
            copy.start()

    def far_share(c):
        for copy in own_block(c):
            copy.wait_recv()
        for copy in far_block(c):
            copy.start()

    PART = 512

    def contract(c):
        for copy in far_block(c):
            copy.wait_recv()
        both = jnp.concatenate([et[c, k] for k in range(4)], axis=1)
        signs = pl.ds(pl.multiple_of(c * AVG, AVG), AVG)

        def piece(owner, p):
            start = pl.multiple_of(owner * half + p * PART, PART)
            x = xg[:, :, :, :, pl.ds(start, PART)].reshape(4 * tokens, PART)
            sums = jnp.dot(both, x, preferred_element_type=F32)
            curv = sums[AVG:] * pt[signs, pl.ds(start, PART)].astype(F32)
            return sums[:AVG] * grad_scale, jnp.sum(curv, axis=0, keepdims=True) * curv_scale

        def put_means(ref, p, means):
            for k in range(PART // 128):
                ref[p * (PART // 128) + k:p * (PART // 128) + k + 1, :] = means[:, k * 128:(k + 1) * 128]

        for p in range(half // PART):
            gradient, means = piece(1 - core, p)
            g_send[c, :, p * PART:(p + 1) * PART] = gradient.astype(BF)
            put_means(m_send.at[c], p, means)
        for copy in twin_block(c):
            copy.start()
        for p in range(half // PART):
            gradient, means = piece(core, p)
            g_own[c % 2, :, p * PART:(p + 1) * PART] = gradient
            put_means(m_own.at[c % 2], p, means)

    def reduce_twin(c):
        for copy in twin_block(c):
            copy.wait_recv()
        h_send[c] = (g_own[c % 2] + g_recv[c].astype(F32)).astype(BF)
        n_send[c] = m_own[c % 2] + m_recv[c]
        for copy in z_block(c):
            copy.start()

    def divide(c):
        for copy in z_block(c):
            copy.wait_recv()
        means = n_send[c] + n_recv[c]
        denom = jnp.maximum(jnp.abs(means), 0.25)
        for k in range(half // 128):
            lanes = slice(k * 128, (k + 1) * 128)
            gradient = h_send[c, :, lanes].astype(F32) + h_recv[c, :, lanes].astype(F32)
            stage[c, lanes, :] = (gradient / denom[k:k + 1, :]).T.astype(BF)
        for copy in result(c):
            copy.start()

    LAG = 7

    def main(t, carry):
        @pl.when(t < nc)
        def _():
            share(t)

        @pl.when((t >= 1) & (t < nc + 1))
        def _():
            far_share(t - 1)

        @pl.when((t >= 2) & (t < nc + 2))
        def _():
            contract(t - 2)

        @pl.when((t >= 3) & (t < nc + 3))
        def _():
            reduce_twin(t - 3)

        @pl.when(t >= LAG)
        def _():
            divide(t - LAG)

        return carry

    lax.fori_loop(0, nc + LAG, main, 0)

    for copy in sent:
        copy.wait_send()
    for group in range(len(GROUPS)):
        for copy in first_hop(group) + second_hop(group):
            copy.wait_send()

    def drain(c, carry):
        for copy in own_block(c) + far_block(c) + twin_block(c) + z_block(c):
            copy.wait_send()
        there, here = result(c)
        there.wait()
        here.wait()
        return carry

    lax.fori_loop(0, nc, drain, 0)


def shards(activations, target, weight, probe_codes):
    share, rows = activations.shape
    cols = weight.shape[1]
    nc = cols // AVG
    tokens_micro = share * lax.axis_size("row")
    total = tokens_micro * lax.axis_size("rep")
    x = activations.reshape(4, 2, SUB, rows)
    y = target.reshape(2, 4, 2, SUB, cols)
    half = rows // 2
    vmem = pltpu.VMEM
    dma = pltpu.SemaphoreType.DMA
    return pl.pallas_call(
        functools.partial(kernel, 1.0 / math.sqrt(total), 1.0 / total / AVG),
        out_shape=jax.ShapeDtypeStruct((rows, cols), BF),
        in_specs=[pl.BlockSpec(memory_space=pltpu.SMEM)] + [pl.BlockSpec(memory_space=pl.ANY)] * 3,
        out_specs=pl.BlockSpec(memory_space=pl.ANY),
        scratch_shapes=[
            vmem((4, 8, 2, SUB, rows), BF),
            vmem((rows, cols), BF),
            vmem((2, 4, 2, SUB, cols), BF),
            vmem((cols, rows), BF),
            vmem((8, 2, SUB, 2 * cols), F32),
            vmem((8, 2, SUB, cols), F32),
            vmem((8, 2, SUB, cols), F32),
            vmem((8, 2, SUB, 2 * cols), BF),
            vmem((8, 2, SUB, 2 * cols), BF),
            vmem((8, 2, SUB, cols), BF),
            vmem((8, 2, SUB, cols), BF),
            vmem((8, 2, SUB, 2 * cols), BF),
            vmem((8, 2, SUB, 2 * cols), BF),
            vmem((8, 2, SUB, cols), BF),
            vmem((8, 2, SUB, cols), BF),
            vmem((nc, 4, 2 * AVG, 256), BF),
            vmem((2, AVG, half), F32),
            vmem((2, 8, 128), F32),
            vmem((nc, AVG, half), BF),
            vmem((nc, 8, 128), F32),
            vmem((nc, AVG, half), BF),
            vmem((nc, 8, 128), F32),
            vmem((nc, AVG, half), BF),
            vmem((nc, 8, 128), F32),
            vmem((nc, AVG, half), BF),
            vmem((nc, 8, 128), F32),
            vmem((nc, half, AVG), BF),
            dma((3,)),
            dma((14,)),
            dma((8, 2)),
            dma((4, 6)),
            dma((4, 6)),
            dma((4, nc)),
            dma((4, nc)),
            dma((2, nc)),
            dma((2, nc)),
            dma((2, nc)),
            dma((2, nc)),
            dma((nc,)),
            dma((nc,)),
            dma((nc,)),
        ],
        compiler_params=pltpu.CompilerParams(
            collective_id=0, has_side_effects=True, vmem_limit_bytes=62 * 1024 * 1024
        ),
    )(probe_codes, x, y, weight)


def solution(mesh):
    placed = (P(("rep", "row"), "col"), P(("rep", "col"), "row"), P("col", "row"), P("col", "row"))
    return jax.shard_map(
        shards, mesh=mesh, in_specs=placed, out_specs=P("col", "row"), check_vma=False
    )
```

```python
import functools
import math

import jax
import jax.numpy as jnp
from jax import lax
from jax.experimental import pallas as pl
from jax.experimental.pallas import tpu as pltpu
from jax.sharding import PartitionSpec as P

MESH = pl.DeviceIdType.MESH
BF = jnp.bfloat16
F32 = jnp.float32
AVG = 128
SUB = 16
ERR, TAN = 0, 1
GROUPS = ((0, 2), (2, 5), (5, 8), (8, 11), (11, 14), (14, 16))


def unit(slot, part):
    return part if slot == 0 else 2 + 3 * part + slot - 1 if slot < 4 else 2 * slot + part


SLOTS = {unit(slot, part): (slot, part) for slot in range(8) for part in range(2)}


def wrapped(value):
    return (value + 2**31) % 2**32 - 2**31


def remote(src, dst, send, recv, peer):
    return pltpu.make_async_remote_copy(
        src_ref=src, dst_ref=dst, send_sem=send, recv_sem=recv,
        device_id=peer, device_id_type=MESH,
    )


def kernel(
    grad_scale, curv_scale, code_ref, x_hbm, y_hbm, w_hbm, out_hbm,
    xg, w, y, pt, own, hold_p, hold_m, sb_p, sb_m, s2_p, s2_m, rb_p, rb_m, r2_p, r2_m,
    et, g_own, m_own, g_send, m_send, g_recv, m_recv, h_send, n_send, h_recv, n_recv, stage,
    load_sem, xs, xr, rs_s, rs_r, ag_s, ag_r, co_s, co_r, zs, zr, fs, fr, ls,
):
    rep, row, col = lax.axis_index("rep"), lax.axis_index("row"), lax.axis_index("col")
    plane, ypos = row // 4, row % 4
    core = rep % 2
    right, left = (col + 1) % 4, (col + 3) % 4
    to_right, to_left = {"col": right}, {"col": left}
    up, down = {"row": plane * 4 + (ypos + 1) % 4}, {"row": plane * 4 + (ypos + 3) % 4}
    across = {"row": (row + 4) % 8}
    twin = {"rep": rep - core + (1 - core)}
    zmate = {"rep": (rep + 2) % 4}
    rows, cols = w.shape
    nc = cols // AVG
    half = rows // 2
    mid = cols // 2

    loads = [
        pltpu.make_async_copy(x_hbm, xg.at[:, 0:2], load_sem.at[0]),
        pltpu.make_async_copy(w_hbm, w, load_sem.at[1]),
        pltpu.make_async_copy(y_hbm, y, load_sem.at[2]),
    ]
    for load in loads:
        load.start()

    barrier = pltpu.get_barrier_semaphore()
    peers = (to_right, to_left, up, down, across, twin, zmate)
    for peer in peers:
        pl.semaphore_signal(barrier, inc=1, device_id=peer, device_id_type=MESH)
    pl.semaphore_wait(barrier, len(peers))
    loads[0].wait()

    sent = []

    def pass_on(slot, part, peer, landing, share=None):
        k = len(sent)
        lo, hi, semaphore = (0, 4, unit(landing, part)) if share is None else (2 * share, 2 * share + 2, 16 + share)
        copy = remote(
            xg.at[lo:hi, unit(slot, part)], xg.at[lo:hi, unit(landing, part)], xs.at[k], xr.at[semaphore], peer
        )
        copy.start()
        sent.append(copy)

    def arrived(slot, part, share=None):
        u = unit(slot, part)
        lo, hi, semaphore = (0, 4, u) if share is None else (2 * share, 2 * share + 2, 16 + share)
        remote(xg.at[lo:hi, u], xg.at[lo:hi, u], xs.at[0], xr.at[semaphore], across).wait_recv()

    for part in range(2):
        pass_on(0, part, across, 1)
        pass_on(0, part, up, 3)
        pass_on(0, part, down, 2)

    loads[1].wait()
    loads[2].wait()

    slot_rows = []
    other = 1 - plane
    for pl_, dy in ((plane, 0), (other, 0), (plane, 1), (plane, 3), (plane, 2), (other, 1), (other, 3), (other, 2)):
        slot_rows.append(pl_ * 4 + (ypos + dy) % 4)

    def members(group):
        lo, hi = GROUPS[group]
        pieces = [xg[(col + k) % 4, lo:hi].reshape((hi - lo) * SUB, rows) for k in range(4)]
        return jnp.concatenate(pieces, axis=0)

    def put(ref, kind, group, lanes, value):
        lo, hi = GROUPS[group]
        ref[kind, lo:hi, :, lanes] = value.reshape(hi - lo, SUB, value.shape[-1])

    def get(ref, kind, group, lanes):
        lo, hi = GROUPS[group]
        value = ref[kind, lo:hi, :, lanes]
        return value.reshape((hi - lo) * SUB, value.shape[-1])

    BLOCK = 256

    def sums_of(kind, group, lanes):
        n = (GROUPS[group][1] - GROUPS[group][0]) * SUB
        if kind == TAN:
            sums = lax.dot_general(
                members(group), pt[lanes, :], (((1,), (1,)), ((), ())), preferred_element_type=F32
            )
            return [sums[k * n:(k + 1) * n] for k in range(4)]
        sums = jnp.dot(members(group), w[:, lanes], preferred_element_type=F32)
        parts = []
        for k in range(4):
            wanted = []
            for u in range(*GROUPS[group]):
                s, h = SLOTS[u]
                mine = (slot_rows[s] // 2 == col).astype(F32)
                wanted.append(y[slot_rows[s] % 2, (col + k) % 4, h, :, lanes].astype(F32) * mine)
            parts.append(sums[k * n:(k + 1) * n] - jnp.concatenate(wanted, axis=0))
        return parts

    def partial(kind, group):
        def low(j, carry):
            lanes = pl.ds(pl.multiple_of(j * BLOCK, BLOCK), BLOCK)
            parts = sums_of(kind, group, lanes)
            put(own, kind, group, lanes, parts[0])
            put(hold_p, kind, group, lanes, parts[1])
            put(sb_p, kind, group, lanes, parts[2].astype(BF))
            put(sb_m, kind, group, lanes, parts[3].astype(BF))
            return carry

        def high(j, carry):
            lanes = pl.ds(pl.multiple_of(j * BLOCK + mid, BLOCK), BLOCK)
            parts = sums_of(kind, group, lanes)
            put(own, kind, group, lanes, parts[0])
            put(sb_p, kind, group, lanes, parts[1].astype(BF))
            put(sb_m, kind, group, lanes, parts[2].astype(BF))
            put(hold_m, kind, group, pl.ds(pl.multiple_of(j * BLOCK, BLOCK), BLOCK), parts[3])
            return carry

        lax.fori_loop(0, mid // BLOCK, low, 0)
        lax.fori_loop(0, mid // BLOCK, high, 0)
        for copy in first_hop(kind, group):
            copy.start()

    def hop(kind, group, number, source, target, peer):
        lo, hi = GROUPS[group]
        return remote(
            source.at[kind, lo:hi], target.at[kind, lo:hi],
            rs_s.at[kind, number, group], rs_r.at[kind, number, group], peer,
        )

    def first_hop(kind, group):
        return [hop(kind, group, 0, sb_p, rb_p, to_right), hop(kind, group, 1, sb_m, rb_m, to_left)]

    def second_hop(kind, group):
        return [hop(kind, group, 2, s2_p, r2_p, to_right), hop(kind, group, 3, s2_m, r2_m, to_left)]

    def relay(kind, group):
        low, high, every = slice(0, mid), slice(mid, cols), slice(0, mid)
        first, second = first_hop(kind, group), second_hop(kind, group)
        first[0].wait_recv()
        put(s2_p, kind, group, every, (get(hold_p, kind, group, every) + get(rb_p, kind, group, low).astype(F32)).astype(BF))
        second[0].start()
        first[1].wait_recv()
        put(s2_m, kind, group, every, (get(hold_m, kind, group, every) + get(rb_m, kind, group, high).astype(F32)).astype(BF))
        second[1].start()

    def reduced(kind):
        for group in range(len(GROUPS)):
            for copy in second_hop(kind, group):
                copy.wait_recv()

    def probe_signs():
        code = code_ref[0, 0] * 1013904223
        lane = lax.broadcasted_iota(jnp.int32, (SUB, 512), 1) * 1664525
        sub = lax.broadcasted_iota(jnp.int32, (SUB, 512), 0) * 22695477
        base = lane + sub + code

        def step(j, carry):
            for i in range(rows // 512):
                mixed = base + (j * (SUB * 22695477) + wrapped(i * 512 * 1664525))
                mixed = mixed ^ mixed >> 15 & 131071
                mixed = mixed * 1274126177
                mixed = mixed ^ mixed >> 13 & 524287
                parity = mixed >> 7 & 1
                pt[pl.ds(pl.multiple_of(j * SUB, SUB), SUB), i * 512:(i + 1) * 512] = (
                    (1 - 2 * parity).astype(F32).astype(BF)
                )
            return carry

        lax.fori_loop(0, cols // SUB, step, 0)

    partial(ERR, 0)
    probe_signs()
    partial(TAN, 0)

    for s in (1, 2, 3):
        arrived(s, 0)
    pass_on(3, 0, up, 4)
    pass_on(2, 0, across, 5)
    pass_on(1, 0, up, 6)
    partial(ERR, 1)
    relay(ERR, 0)
    partial(TAN, 1)
    relay(TAN, 0)

    for s in (1, 2, 3):
        arrived(s, 1)
    pass_on(2, 1, down, 4)
    pass_on(3, 1, across, 6)
    pass_on(1, 1, down, 5)
    partial(ERR, 2)
    relay(ERR, 1)
    partial(TAN, 2)
    relay(TAN, 1)

    arrived(4, 0)
    pass_on(4, 0, across, 7)
    arrived(5, 0)
    arrived(4, 1)
    partial(ERR, 3)
    relay(ERR, 2)
    partial(TAN, 3)
    relay(TAN, 2)

    arrived(6, 0)
    arrived(6, 1)
    pass_on(6, 1, up, 7, 0)
    arrived(5, 1)
    pass_on(5, 1, down, 7, 1)
    partial(ERR, 4)
    relay(ERR, 3)
    relay(TAN, 3)

    arrived(7, 0)
    arrived(7, 1, 0)
    arrived(7, 1, 1)
    partial(ERR, 5)
    relay(ERR, 4)
    partial(TAN, 4)
    relay(ERR, 5)
    partial(TAN, 5)
    relay(TAN, 4)
    reduced(ERR)

    def own_block(kind, c):
        area = et.at[kind, c, col]
        return [
            remote(area, area, ag_s.at[kind, 0, c], ag_r.at[kind, 0, c], to_right),
            remote(area, area, ag_s.at[kind, 1, c], ag_r.at[kind, 1, c], to_left),
        ]

    def far_block(kind, c):
        first, second = slice(0, AVG // 2), slice(AVG // 2, AVG)
        low, high = et.at[kind, c, left, first], et.at[kind, c, right, second]
        return [
            remote(low, low, ag_s.at[kind, 2, c], ag_r.at[kind, 2, c], to_right),
            remote(high, high, ag_s.at[kind, 3, c], ag_r.at[kind, 3, c], to_left),
        ]

    def twin_block(c):
        return [remote(g_send.at[c], g_recv.at[c], co_s.at[0, c], co_r.at[0, c], twin)]

    def twin_means(c):
        return [remote(m_send.at[c], m_recv.at[c], co_s.at[1, c], co_r.at[1, c], twin)]

    def z_block(c):
        return [remote(h_send.at[c], h_recv.at[c], zs.at[0, c], zr.at[0, c], zmate)]

    def z_means(c):
        return [remote(n_send.at[c], n_recv.at[c], zs.at[1, c], zr.at[1, c], zmate)]

    def result(c):
        area = out_hbm.at[
            pl.ds(pl.multiple_of(core * half, half), half), pl.ds(pl.multiple_of(c * AVG, AVG), AVG)
        ]
        return remote(stage.at[c], area, fs.at[c], fr.at[c], twin), pltpu.make_async_copy(
            stage.at[c], area, ls.at[c]
        )

    units = own.shape[1]
    tokens = units * SUB

    def share(kind, c):
        lanes = pl.ds(pl.multiple_of(c * AVG, AVG), AVG)
        within = pl.ds(pl.multiple_of(c % (nc // 2) * AVG, AVG), AVG)

        def all_of(ref, lanes):
            return ref[kind, :, :, lanes].reshape(tokens, AVG).astype(F32)

        def finish(direct, relayed):
            total = all_of(own, lanes) + all_of(direct, lanes) + all_of(relayed, within)
            et[kind, c, col] = total.T.astype(BF)

        @pl.when(c < nc // 2)
        def _():
            finish(rb_m, r2_p)

        @pl.when(c >= nc // 2)
        def _():
            finish(rb_p, r2_m)

        for copy in own_block(kind, c):
            copy.start()

    def far_share(kind, c):
        own_copies, far_copies = own_block(kind, c), far_block(kind, c)
        for mine, theirs in zip(own_copies, far_copies):
            mine.wait_recv()
            theirs.start()

    PART = 512

    def whole(kind, c):
        for copy in far_block(kind, c):
            copy.wait_recv()
        return jnp.concatenate([et[kind, c, k] for k in range(4)], axis=1)

    def product(block, owner, p):
        start = pl.multiple_of(owner * half + p * PART, PART)
        x = xg[:, :, :, pl.ds(start, PART)].reshape(4 * tokens, PART)
        return jnp.dot(block, x, preferred_element_type=F32), pl.ds(start, PART)

    def contract(c):
        errors = whole(ERR, c)
        for p in range(half // PART):
            g_send[c, :, p * PART:(p + 1) * PART] = (product(errors, 1 - core, p)[0] * grad_scale).astype(BF)
        for copy in twin_block(c):
            copy.start()
        for p in range(half // PART):
            g_own[c % 2, :, p * PART:(p + 1) * PART] = product(errors, core, p)[0] * grad_scale

    def curvature(c):
        tangents = whole(TAN, c)
        signs = pl.ds(pl.multiple_of(c * AVG, AVG), AVG)

        def means(ref, owner):
            for p in range(half // PART):
                sums, lanes = product(tangents, owner, p)
                mean = jnp.sum(sums * pt[signs, lanes].astype(F32), axis=0, keepdims=True) * curv_scale
                for k in range(PART // 128):
                    at = p * (PART // 128) + k
                    ref[at:at + 1, :] = mean[:, k * 128:(k + 1) * 128]

        means(m_send.at[c], 1 - core)
        for copy in twin_means(c):
            copy.start()
        means(m_own.at[c % 2], core)

    def reduce_twin(c):
        for copy in twin_block(c):
            copy.wait_recv()
        h_send[c] = (g_own[c % 2] + g_recv[c].astype(F32)).astype(BF)
        for copy in z_block(c):
            copy.start()

    def reduce_means(c):
        for copy in twin_means(c):
            copy.wait_recv()
        n_send[c] = m_own[c % 2] + m_recv[c]
        for copy in z_means(c):
            copy.start()

    def divide(c):
        for copy in z_block(c) + z_means(c):
            copy.wait_recv()
        means = n_send[c] + n_recv[c]
        denom = jnp.maximum(jnp.abs(means), 0.25)
        for k in range(half // 128):
            lanes = slice(k * 128, (k + 1) * 128)
            gradient = h_send[c, :, lanes].astype(F32) + h_recv[c, :, lanes].astype(F32)
            stage[c, lanes, :] = (gradient / denom[k:k + 1, :]).T.astype(BF)
        for copy in result(c):
            copy.start()

    LAG = 7

    def main(t, carry):
        def when(lag):
            return pl.when((t >= lag) & (t < nc + lag))

        @when(0)
        def _():
            share(ERR, t)

        @pl.when(t == 0)
        def _():
            relay(TAN, 5)

        @when(1)
        def _():
            far_share(ERR, t - 1)

        @when(2)
        def _():
            contract(t - 2)

        @pl.when(t == 2)
        def _():
            reduced(TAN)

        @when(2)
        def _():
            share(TAN, t - 2)
            reduce_twin(t - 2)

        @when(3)
        def _():
            far_share(TAN, t - 3)

        @when(4)
        def _():
            curvature(t - 4)

        @when(LAG)
        def _():
            divide(t - LAG)

        @when(4)
        def _():
            reduce_means(t - 4)

        return carry

    lax.fori_loop(0, nc + LAG, main, 0)

    for copy in sent:
        copy.wait_send()
    for kind in (ERR, TAN):
        for group in range(len(GROUPS)):
            for copy in first_hop(kind, group) + second_hop(kind, group):
                copy.wait_send()

    def drain(c, carry):
        for kind in (ERR, TAN):
            for copy in own_block(kind, c) + far_block(kind, c):
                copy.wait_send()
        for copy in twin_block(c) + twin_means(c) + z_block(c) + z_means(c):
            copy.wait_send()
        there, here = result(c)
        there.wait()
        here.wait()
        return carry

    lax.fori_loop(0, nc, drain, 0)


def shards(activations, target, weight, probe_codes):
    share, rows = activations.shape
    cols = weight.shape[1]
    nc = cols // AVG
    tokens_micro = share * lax.axis_size("row")
    total = tokens_micro * lax.axis_size("rep")
    x = activations.reshape(4, 2, SUB, rows)
    y = target.reshape(2, 4, 2, SUB, cols)
    half = rows // 2
    vmem = pltpu.VMEM
    dma = pltpu.SemaphoreType.DMA
    return pl.pallas_call(
        functools.partial(kernel, 1.0 / math.sqrt(total), 1.0 / total / AVG),
        out_shape=jax.ShapeDtypeStruct((rows, cols), BF),
        in_specs=[pl.BlockSpec(memory_space=pltpu.SMEM)] + [pl.BlockSpec(memory_space=pl.ANY)] * 3,
        out_specs=pl.BlockSpec(memory_space=pl.ANY),
        scratch_shapes=[
            vmem((4, 16, SUB, rows), BF),
            vmem((rows, cols), BF),
            vmem((2, 4, 2, SUB, cols), BF),
            vmem((cols, rows), BF),
            vmem((2, 16, SUB, cols), F32),
            vmem((2, 16, SUB, cols // 2), F32),
            vmem((2, 16, SUB, cols // 2), F32),
            vmem((2, 16, SUB, cols), BF),
            vmem((2, 16, SUB, cols), BF),
            vmem((2, 16, SUB, cols // 2), BF),
            vmem((2, 16, SUB, cols // 2), BF),
            vmem((2, 16, SUB, cols), BF),
            vmem((2, 16, SUB, cols), BF),
            vmem((2, 16, SUB, cols // 2), BF),
            vmem((2, 16, SUB, cols // 2), BF),
            vmem((2, nc, 4, AVG, 256), BF),
            vmem((2, AVG, half), F32),
            vmem((2, 8, 128), F32),
            vmem((nc, AVG, half), BF),
            vmem((nc, 8, 128), F32),
            vmem((nc, AVG, half), BF),
            vmem((nc, 8, 128), F32),
            vmem((nc, AVG, half), BF),
            vmem((nc, 8, 128), F32),
            vmem((nc, AVG, half), BF),
            vmem((nc, 8, 128), F32),
            vmem((nc, half, AVG), BF),
            dma((3,)),
            dma((15,)),
            dma((18,)),
            dma((2, 4, 6)),
            dma((2, 4, 6)),
            dma((2, 4, nc)),
            dma((2, 4, nc)),
            dma((2, nc)),
            dma((2, nc)),
            dma((2, nc)),
            dma((2, nc)),
            dma((nc,)),
            dma((nc,)),
            dma((nc,)),
        ],
        compiler_params=pltpu.CompilerParams(
            collective_id=0, has_side_effects=True, vmem_limit_bytes=62 * 1024 * 1024
        ),
    )(probe_codes, x, y, weight)


def solution(mesh):
    placed = (P(("rep", "row"), "col"), P(("rep", "col"), "row"), P("col", "row"), P("col", "row"))
    return jax.shard_map(
        shards, mesh=mesh, in_specs=placed, out_specs=P("col", "row"), check_vma=False
    )
```

```python
import functools
import math

import jax
import jax.numpy as jnp
from jax import lax
from jax.experimental import pallas as pl
from jax.experimental.pallas import tpu as pltpu
from jax.sharding import PartitionSpec as P

MESH = pl.DeviceIdType.MESH
BF = jnp.bfloat16
F32 = jnp.float32
AVG = 128
SUB = 16
ERR, TAN = 0, 1
GROUPS = ((0, 2), (2, 5), (5, 8), (8, 11), (11, 14), (14, 16))


def unit(slot, part):
    return part if slot == 0 else 2 + 3 * part + slot - 1 if slot < 4 else 2 * slot + part


SLOTS = {unit(slot, part): (slot, part) for slot in range(8) for part in range(2)}


def wrapped(value):
    return (value + 2**31) % 2**32 - 2**31


def remote(src, dst, send, recv, peer):
    return pltpu.make_async_remote_copy(
        src_ref=src, dst_ref=dst, send_sem=send, recv_sem=recv,
        device_id=peer, device_id_type=MESH,
    )


def kernel(
    grad_scale, curv_scale, code_ref, x_hbm, y_hbm, w_hbm, out,
    xg, w, y, pt, own, hold_p, hold_m, sb_p, sb_m, s2_p, s2_m, rb_p, rb_m, r2_p, r2_m,
    et, g_own, m_own, g_send, m_send, g_recv, m_recv, h_send, n_send, h_recv, n_recv,
    load_sem, xs, xr, rs_s, rs_r, ag_s, ag_r, co_s, co_r, zs, zr, fs, fr,
):
    rep, row, col = lax.axis_index("rep"), lax.axis_index("row"), lax.axis_index("col")
    plane, ypos = row // 4, row % 4
    core = rep % 2
    right, left = (col + 1) % 4, (col + 3) % 4
    to_right, to_left, to_far = {"col": right}, {"col": left}, {"col": (col + 2) % 4}
    up, down = {"row": plane * 4 + (ypos + 1) % 4}, {"row": plane * 4 + (ypos + 3) % 4}
    across = {"row": (row + 4) % 8}
    twin = {"rep": rep - core + (1 - core)}
    zmate = {"rep": (rep + 2) % 4}
    rows, cols = w.shape
    nc = cols // AVG
    half = rows // 2
    mid = cols // 2

    loads = [
        pltpu.make_async_copy(x_hbm, xg.at[:, 0:2], load_sem.at[0]),
        pltpu.make_async_copy(w_hbm, w, load_sem.at[1]),
        pltpu.make_async_copy(y_hbm, y, load_sem.at[2]),
    ]
    for load in loads:
        load.start()

    barrier = pltpu.get_barrier_semaphore()
    peers = (to_right, to_left, to_far, up, down, across, twin, zmate)
    for peer in peers:
        pl.semaphore_signal(barrier, inc=1, device_id=peer, device_id_type=MESH)
    pl.semaphore_wait(barrier, len(peers))
    loads[0].wait()

    sent = []

    def pass_on(slot, part, peer, landing, share=None):
        k = len(sent)
        lo, hi, semaphore = (0, 4, unit(landing, part)) if share is None else (2 * share, 2 * share + 2, 16 + share)
        copy = remote(
            xg.at[lo:hi, unit(slot, part)], xg.at[lo:hi, unit(landing, part)], xs.at[k], xr.at[semaphore], peer
        )
        copy.start()
        sent.append(copy)

    def arrived(slot, part, share=None):
        u = unit(slot, part)
        lo, hi, semaphore = (0, 4, u) if share is None else (2 * share, 2 * share + 2, 16 + share)
        remote(xg.at[lo:hi, u], xg.at[lo:hi, u], xs.at[0], xr.at[semaphore], across).wait_recv()

    for part in range(2):
        pass_on(0, part, across, 1)
        pass_on(0, part, up, 3)
        pass_on(0, part, down, 2)

    loads[1].wait()
    loads[2].wait()

    slot_rows = []
    other = 1 - plane
    for pl_, dy in ((plane, 0), (other, 0), (plane, 1), (plane, 3), (plane, 2), (other, 1), (other, 3), (other, 2)):
        slot_rows.append(pl_ * 4 + (ypos + dy) % 4)

    def members(group):
        lo, hi = GROUPS[group]
        pieces = [xg[(col + k) % 4, lo:hi].reshape((hi - lo) * SUB, rows) for k in range(4)]
        return jnp.concatenate(pieces, axis=0)

    def put(ref, kind, group, lanes, value):
        lo, hi = GROUPS[group]
        ref[kind, lo:hi, :, lanes] = value.reshape(hi - lo, SUB, value.shape[-1])

    def get(ref, kind, group, lanes):
        lo, hi = GROUPS[group]
        value = ref[kind, lo:hi, :, lanes]
        return value.reshape((hi - lo) * SUB, value.shape[-1])

    BLOCK = 256

    def sums_of(kind, group, lanes):
        n = (GROUPS[group][1] - GROUPS[group][0]) * SUB
        if kind == TAN:
            sums = lax.dot_general(
                members(group), pt[lanes, :], (((1,), (1,)), ((), ())), preferred_element_type=F32
            )
            return [sums[k * n:(k + 1) * n] for k in range(4)]
        sums = jnp.dot(members(group), w[:, lanes], preferred_element_type=F32)
        parts = []
        for k in range(4):
            wanted = []
            for u in range(*GROUPS[group]):
                s, h = SLOTS[u]
                mine = (slot_rows[s] // 2 == col).astype(F32)
                wanted.append(y[slot_rows[s] % 2, (col + k) % 4, h, :, lanes].astype(F32) * mine)
            parts.append(sums[k * n:(k + 1) * n] - jnp.concatenate(wanted, axis=0))
        return parts

    def partial(kind, group, hold=False):
        def low(j, carry):
            lanes = pl.ds(pl.multiple_of(j * BLOCK, BLOCK), BLOCK)
            parts = sums_of(kind, group, lanes)
            put(own, kind, group, lanes, parts[0])
            put(hold_p, kind, group, lanes, parts[1])
            put(sb_p, kind, group, lanes, parts[2].astype(BF))
            put(sb_m, kind, group, lanes, parts[3].astype(BF))
            return carry

        def high(j, carry):
            lanes = pl.ds(pl.multiple_of(j * BLOCK + mid, BLOCK), BLOCK)
            parts = sums_of(kind, group, lanes)
            put(own, kind, group, lanes, parts[0])
            put(sb_p, kind, group, lanes, parts[1].astype(BF))
            put(sb_m, kind, group, lanes, parts[2].astype(BF))
            put(hold_m, kind, group, pl.ds(pl.multiple_of(j * BLOCK, BLOCK), BLOCK), parts[3])
            return carry

        lax.fori_loop(0, mid // BLOCK, low, 0)
        lax.fori_loop(0, mid // BLOCK, high, 0)
        if not hold:
            for copy in first_hop(kind, group):
                copy.start()

    def hop(kind, group, number, source, target, peer):
        lo, hi = GROUPS[group]
        return remote(
            source.at[kind, lo:hi], target.at[kind, lo:hi],
            rs_s.at[kind, number, group], rs_r.at[kind, number, group], peer,
        )

    def first_hop(kind, group):
        return [hop(kind, group, 0, sb_p, rb_p, to_right), hop(kind, group, 1, sb_m, rb_m, to_left)]

    def second_hop(kind, group):
        return [hop(kind, group, 2, s2_p, r2_p, to_right), hop(kind, group, 3, s2_m, r2_m, to_left)]

    def relay(kind, group):
        low, high, every = slice(0, mid), slice(mid, cols), slice(0, mid)
        first, second = first_hop(kind, group), second_hop(kind, group)
        first[0].wait_recv()
        put(s2_p, kind, group, every, (get(hold_p, kind, group, every) + get(rb_p, kind, group, low).astype(F32)).astype(BF))
        second[0].start()
        first[1].wait_recv()
        put(s2_m, kind, group, every, (get(hold_m, kind, group, every) + get(rb_m, kind, group, high).astype(F32)).astype(BF))
        second[1].start()

    LAST = len(GROUPS) - 1

    def lane_hop(kind, number, source, target, peer, lanes):
        lo, hi = GROUPS[LAST]
        return remote(
            source.at[kind, lo:hi, :, lanes], target.at[kind, lo:hi, :, lanes],
            rs_s.at[kind, number, LAST], rs_r.at[kind, number, LAST], peer,
        )

    def straight(kind, high):
        lanes = slice(mid, cols) if high else slice(0, mid)
        far = hop(kind, LAST, 3, s2_m, r2_m, to_far) if high else hop(kind, LAST, 2, s2_p, r2_p, to_far)
        return [
            lane_hop(kind, 4 if high else 0, sb_p, rb_p, to_right, lanes),
            lane_hop(kind, 5 if high else 1, sb_m, rb_m, to_left, lanes),
            far,
        ]

    def partial_last(kind, hold=False):
        def low(j, carry):
            lanes = pl.ds(pl.multiple_of(j * BLOCK, BLOCK), BLOCK)
            parts = sums_of(kind, LAST, lanes)
            put(own, kind, LAST, lanes, parts[0])
            put(sb_p, kind, LAST, lanes, parts[1].astype(BF))
            put(s2_p, kind, LAST, lanes, parts[2].astype(BF))
            put(sb_m, kind, LAST, lanes, parts[3].astype(BF))
            return carry

        def high(j, carry):
            lanes = pl.ds(pl.multiple_of(j * BLOCK + mid, BLOCK), BLOCK)
            parts = sums_of(kind, LAST, lanes)
            put(own, kind, LAST, lanes, parts[0])
            put(sb_p, kind, LAST, lanes, parts[1].astype(BF))
            put(s2_m, kind, LAST, pl.ds(pl.multiple_of(j * BLOCK, BLOCK), BLOCK), parts[2].astype(BF))
            put(sb_m, kind, LAST, lanes, parts[3].astype(BF))
            return carry

        lax.fori_loop(0, mid // BLOCK, low, 0)
        if not hold:
            for copy in straight(kind, False):
                copy.start()
        lax.fori_loop(0, mid // BLOCK, high, 0)
        if not hold:
            for copy in straight(kind, True):
                copy.start()

    def reduced(kind, high):
        for group in range(LAST):
            second_hop(kind, group)[1 if high else 0].wait_recv()
        for copy in straight(kind, high):
            copy.wait_recv()
        lanes, ref = (slice(mid, cols), rb_m) if high else (slice(0, mid), rb_p)
        put(own, kind, LAST, lanes, get(own, kind, LAST, lanes) + get(ref, kind, LAST, lanes).astype(F32))

    def probe_signs():
        code = code_ref[0, 0] * 1013904223
        lane = lax.broadcasted_iota(jnp.int32, (SUB, 512), 1) * 1664525
        sub = lax.broadcasted_iota(jnp.int32, (SUB, 512), 0) * 22695477
        base = lane + sub + code

        def step(j, carry):
            for i in range(rows // 512):
                mixed = base + (j * (SUB * 22695477) + wrapped(i * 512 * 1664525))
                mixed = mixed ^ mixed >> 15 & 131071
                mixed = mixed * 1274126177
                mixed = mixed ^ mixed >> 13 & 524287
                parity = mixed >> 7 & 1
                pt[pl.ds(pl.multiple_of(j * SUB, SUB), SUB), i * 512:(i + 1) * 512] = (
                    (1 - 2 * parity).astype(F32).astype(BF)
                )
            return carry

        lax.fori_loop(0, cols // SUB, step, 0)

    partial(ERR, 0)
    probe_signs()
    partial(TAN, 0)

    for s in (1, 2, 3):
        arrived(s, 0)
    pass_on(3, 0, up, 4)
    pass_on(2, 0, across, 5)
    pass_on(1, 0, up, 6)
    partial(ERR, 1)
    relay(ERR, 0)
    partial(TAN, 1)
    relay(TAN, 0)

    for s in (1, 2, 3):
        arrived(s, 1)
    pass_on(2, 1, down, 4)
    pass_on(3, 1, across, 6)
    pass_on(1, 1, down, 5)
    partial(ERR, 2)
    relay(ERR, 1)
    partial(TAN, 2)
    relay(TAN, 1)

    arrived(4, 0)
    pass_on(4, 0, across, 7)
    arrived(5, 0)
    arrived(4, 1)
    partial(ERR, 3)
    relay(ERR, 2)
    partial(TAN, 3, hold=True)
    relay(TAN, 2)

    arrived(6, 0)
    arrived(6, 1)
    pass_on(6, 1, up, 7, 0)
    arrived(5, 1)
    pass_on(5, 1, down, 7, 1)
    partial(ERR, 4)
    relay(ERR, 3)

    arrived(7, 0)
    arrived(7, 1, 0)
    arrived(7, 1, 1)
    relay(ERR, 4)
    partial_last(ERR)
    partial(TAN, 4, hold=True)
    reduced(ERR, False)

    def own_block(kind, c):
        area = et.at[kind, c, col]
        return [
            remote(area, area, ag_s.at[kind, 0, c], ag_r.at[kind, 0, c], to_right),
            remote(area, area, ag_s.at[kind, 1, c], ag_r.at[kind, 1, c], to_left),
        ]

    def far_block(kind, c):
        first, second = slice(0, AVG // 2), slice(AVG // 2, AVG)
        low, high = et.at[kind, c, left, first], et.at[kind, c, right, second]
        return [
            remote(low, low, ag_s.at[kind, 2, c], ag_r.at[kind, 2, c], to_right),
            remote(high, high, ag_s.at[kind, 3, c], ag_r.at[kind, 3, c], to_left),
        ]

    def first_block(c):
        first, second = slice(0, AVG // 2), slice(AVG // 2, AVG)
        low, high = et.at[ERR, c, col, first], et.at[ERR, c, col, second]
        return own_block(ERR, c) + [
            remote(low, low, ag_s.at[ERR, 2, c], ag_r.at[ERR, 2, c], to_far),
            remote(high, high, ag_s.at[ERR, 3, c], ag_r.at[ERR, 3, c], to_far),
        ]

    PARTS = 2
    PART = half // PARTS

    def twin_block(c, p):
        return remote(g_send.at[c, p], g_recv.at[c, p], co_s.at[p, c], co_r.at[p, c], twin)

    def twin_means(c):
        return remote(m_send.at[c], m_recv.at[c], co_s.at[PARTS, c], co_r.at[PARTS, c], twin)

    def z_block(c, p):
        return remote(h_send.at[c, p], h_recv.at[c, p], zs.at[p, c], zr.at[p, c], zmate)

    def z_means(c):
        return remote(n_send.at[c], n_recv.at[c], zs.at[PARTS, c], zr.at[PARTS, c], zmate)

    def result(c, p):
        area = out.at[
            pl.ds(pl.multiple_of(core * half + p * PART, PART), PART), pl.ds(pl.multiple_of(c * AVG, AVG), AVG)
        ]
        return remote(area, area, fs.at[p, c], fr.at[p, c], twin)

    units = own.shape[1]
    tokens = units * SUB

    def share(kind, c):
        lanes = pl.ds(pl.multiple_of(c * AVG, AVG), AVG)
        within = pl.ds(pl.multiple_of(c % (nc // 2) * AVG, AVG), AVG)

        def all_of(ref, lanes):
            return ref[kind, :, :, lanes].reshape(tokens, AVG).astype(F32)

        def finish(direct, relayed):
            total = all_of(own, lanes) + all_of(direct, lanes) + all_of(relayed, within)
            et[kind, c, col] = total.T.astype(BF)

        @pl.when(c < nc // 2)
        def _():
            finish(rb_m, r2_p)

        @pl.when(c >= nc // 2)
        def _():
            finish(rb_p, r2_m)

    def send_share(kind, c):
        share(kind, c)
        for copy in own_block(kind, c):
            copy.start()

    def far_share(kind, c):
        own_copies, far_copies = own_block(kind, c), far_block(kind, c)
        for mine, theirs in zip(own_copies, far_copies):
            mine.wait_recv()
            theirs.start()

    def whole(kind, c):
        for copy in far_block(kind, c):
            copy.wait_recv()
        return jnp.concatenate([et[kind, c, k] for k in range(4)], axis=1)

    def product(block, owner, p):
        start = pl.multiple_of(owner * half + p * PART, PART)
        x = xg[:, :, :, pl.ds(start, PART)].reshape(4 * tokens, PART)
        return jnp.dot(block, x, preferred_element_type=F32), pl.ds(start, PART)

    def contract(e, t):
        blocks = [] if e is None else [whole(ERR, e)]
        blocks += [] if t is None else [whole(TAN, t)]
        both = jnp.concatenate(blocks, axis=0)

        def means(sums, lanes, ref, p):
            signs = pl.ds(pl.multiple_of(t * AVG, AVG), AVG)
            mean = jnp.sum(sums * pt[signs, lanes].astype(F32), axis=0, keepdims=True) * curv_scale
            for k in range(PART // 128):
                at = p * (PART // 128) + k
                ref[at:at + 1, :] = mean[:, k * 128:(k + 1) * 128]

        for p in range(PARTS):
            sums, lanes = product(both, 1 - core, p)
            if e is not None:
                g_send[e, p] = (sums[:AVG] * grad_scale).astype(BF)
                twin_block(e, p).start()
            if t is not None:
                means(sums[-AVG:], lanes, m_send.at[t], p)
        if t is not None:
            twin_means(t).start()
        for p in range(PARTS):
            sums, lanes = product(both, core, p)
            if e is not None:
                g_own[p] = sums[:AVG] * grad_scale
            if t is not None:
                means(sums[-AVG:], lanes, m_own, p)

    def reduce_means(t):
        twin_means(t).wait_recv()
        n_send[t] = m_own[...] + m_recv[t]
        z_means(t).start()

    def reduce_twin(e):
        for p in range(PARTS):
            twin_block(e, p).wait_recv()
            h_send[e, p] = (g_own[p] + g_recv[e, p].astype(F32)).astype(BF)

    def divide(c):
        z_means(c).wait_recv()
        means = n_send[c] + n_recv[c]
        denom = jnp.maximum(jnp.abs(means), 0.25)
        columns = pl.ds(pl.multiple_of(c * AVG, AVG), AVG)
        for p in range(PARTS):
            z_block(c, p).wait_recv()
            for k in range(PART // 128):
                lanes = slice(k * 128, (k + 1) * 128)
                at = p * (PART // 128) + k
                gradient = h_send[c, p, :, lanes].astype(F32) + h_recv[c, p, :, lanes].astype(F32)
                out[pl.ds(pl.multiple_of(core * half + at * 128, 128), 128), columns] = (
                    gradient / denom[at:at + 1, :]
                ).T.astype(BF)
            result(c, p).start()

    def z_start(c):
        for p in range(PARTS):
            z_block(c, p).start()

    share(ERR, 0)
    for copy in first_block(0):
        copy.start()
    send_share(ERR, 1)
    send_share(ERR, 2)
    for copy in first_hop(TAN, 3):
        copy.start()
    partial_last(TAN, hold=True)
    for copy in own_block(ERR, 0):
        copy.wait_recv()
    contract(0, None)
    far_share(ERR, 1)
    send_share(ERR, 3)
    reduce_twin(0)
    z_start(0)
    for copy in first_hop(TAN, 4):
        copy.start()
    relay(TAN, 3)

    BACK, LAG = 5, 8

    def main(t, carry):
        def when(lag):
            return pl.when((t >= lag) & (t < nc + lag))

        @pl.when(t + 1 < nc)
        def _():
            far_share(ERR, t + 1)

        @when(BACK - 1)
        def _():
            far_share(TAN, t - (BACK - 1))

        @pl.when(t == 1)
        def _():
            for copy in straight(TAN, False) + straight(TAN, True):
                copy.start()
            reduced(ERR, True)

        @pl.when(t + 3 < nc)
        def _():
            send_share(ERR, t + 3)

        @pl.when((t >= 3) & (t < nc + 2))
        def _():
            send_share(TAN, t - 2)

        @pl.when(t < BACK)
        def _():
            contract(t, None)

        @pl.when((t >= BACK) & (t < nc))
        def _():
            contract(t, t - BACK)

        @pl.when((t >= nc) & (t < nc + BACK))
        def _():
            contract(None, t - BACK)

        @when(BACK)
        def _():
            reduce_means(t - BACK)

        @pl.when(t < nc)
        def _():
            reduce_twin(t)

        @pl.when(t < 6)
        def _():
            z_start(t)

        @pl.when((t == 7) | (t == 9))
        def _():
            z_start((t + 5) // 2)

        @pl.when(t == 1)
        def _():
            relay(TAN, 4)

        @pl.when(t == 2)
        def _():
            reduced(TAN, False)
            reduced(TAN, True)
            send_share(TAN, 0)

        @when(LAG)
        def _():
            divide(t - LAG)

        return carry

    lax.fori_loop(1, nc + LAG, main, 0)

    for copy in sent:
        copy.wait_send()
    for kind in (ERR, TAN):
        for group in range(LAST):
            for copy in first_hop(kind, group) + second_hop(kind, group):
                copy.wait_send()
        for copy in straight(kind, False) + straight(kind, True):
            copy.wait_send()

    def drain(c, carry):
        for kind in (ERR, TAN):
            for copy in own_block(kind, c) + far_block(kind, c):
                copy.wait_send()
        twin_means(c).wait_send()
        z_means(c).wait_send()
        for p in range(PARTS):
            twin_block(c, p).wait_send()
            z_block(c, p).wait_send()
            result(c, p).wait()
        return carry

    lax.fori_loop(0, nc, drain, 0)


def write_out(step, out, sems):
    n = sems.shape[0]
    size = step.shape[0] // n
    copies = [
        pltpu.make_async_copy(step.at[pl.ds(k * size, size)], out.at[pl.ds(k * size, size)], sems.at[k])
        for k in range(n)
    ]
    for copy in copies:
        copy.start()
    for copy in copies:
        copy.wait()


def shards(activations, target, weight, probe_codes):
    share, rows = activations.shape
    cols = weight.shape[1]
    nc = cols // AVG
    tokens_micro = share * lax.axis_size("row")
    total = tokens_micro * lax.axis_size("rep")
    x = activations.reshape(4, 2, SUB, rows)
    y = target.reshape(2, 4, 2, SUB, cols)
    half = rows // 2
    vmem = pltpu.VMEM
    dma = pltpu.SemaphoreType.DMA
    step = pl.pallas_call(
        functools.partial(kernel, 1.0 / math.sqrt(total), 1.0 / total / AVG),
        out_shape=pltpu.VMEM((rows, cols), BF),
        in_specs=[pl.BlockSpec(memory_space=pltpu.SMEM)] + [pl.BlockSpec(memory_space=pltpu.MemorySpace.HBM)] * 3,
        out_specs=pl.BlockSpec(memory_space=pltpu.VMEM),
        scratch_shapes=[
            vmem((4, 16, SUB, rows), BF),
            vmem((rows, cols), BF),
            vmem((2, 4, 2, SUB, cols), BF),
            vmem((cols, rows), BF),
            vmem((2, 16, SUB, cols), F32),
            vmem((2, 16, SUB, cols // 2), F32),
            vmem((2, 16, SUB, cols // 2), F32),
            vmem((2, 16, SUB, cols), BF),
            vmem((2, 16, SUB, cols), BF),
            vmem((2, 16, SUB, cols // 2), BF),
            vmem((2, 16, SUB, cols // 2), BF),
            vmem((2, 16, SUB, cols), BF),
            vmem((2, 16, SUB, cols), BF),
            vmem((2, 16, SUB, cols // 2), BF),
            vmem((2, 16, SUB, cols // 2), BF),
            vmem((2, nc, 4, AVG, 256), BF),
            vmem((2, AVG, half // 2), F32),
            vmem((8, 128), F32),
            vmem((nc, 2, AVG, half // 2), BF),
            vmem((nc, 8, 128), F32),
            vmem((nc, 2, AVG, half // 2), BF),
            vmem((nc, 8, 128), F32),
            vmem((nc, 2, AVG, half // 2), BF),
            vmem((nc, 8, 128), F32),
            vmem((nc, 2, AVG, half // 2), BF),
            vmem((nc, 8, 128), F32),
            dma((3,)),
            dma((15,)),
            dma((18,)),
            dma((2, 6, 6)),
            dma((2, 6, 6)),
            dma((2, 4, nc)),
            dma((2, 4, nc)),
            dma((3, nc)),
            dma((3, nc)),
            dma((3, nc)),
            dma((3, nc)),
            dma((2, nc)),
            dma((2, nc)),
        ],
        compiler_params=pltpu.CompilerParams(
            collective_id=0, has_side_effects=True, vmem_limit_bytes=50 * 1024 * 1024
        ),
    )(probe_codes, *(pltpu.with_memory_space_constraint(v, pltpu.MemorySpace.HBM) for v in (x, y, weight)))
    return pl.pallas_call(
        write_out,
        out_shape=jax.ShapeDtypeStruct((rows, cols), BF),
        in_specs=[pl.BlockSpec(memory_space=pltpu.VMEM)],
        out_specs=pl.BlockSpec(memory_space=pltpu.MemorySpace.HBM),
        scratch_shapes=[dma((4,))],
        compiler_params=pltpu.CompilerParams(vmem_limit_bytes=1024 * 1024),
    )(step)


def solution(mesh):
    placed = (P(("rep", "row"), "col"), P(("rep", "col"), "row"), P("col", "row"), P("col", "row"))
    return jax.shard_map(
        shards, mesh=mesh, in_specs=placed, out_specs=P("col", "row"), check_vma=False
    )
```

```python
import functools
import math

import jax
import jax.numpy as jnp
from jax import lax
from jax.experimental import pallas as pl
from jax.experimental.pallas import tpu as pltpu
from jax.sharding import PartitionSpec as P

MESH = pl.DeviceIdType.MESH
BF = jnp.bfloat16
F32 = jnp.float32
AVG = 128
SUB = 16
ERR, TAN = 0, 1
GROUPS = ((0, 2), (2, 5), (5, 8), (8, 11), (11, 14), (14, 16))


def unit(slot, part):
    return part if slot == 0 else 2 + 3 * part + slot - 1 if slot < 4 else 2 * slot + part


SLOTS = {unit(slot, part): (slot, part) for slot in range(8) for part in range(2)}


def wrapped(value):
    return (value + 2**31) % 2**32 - 2**31


def remote(src, dst, send, recv, peer):
    return pltpu.make_async_remote_copy(
        src_ref=src, dst_ref=dst, send_sem=send, recv_sem=recv,
        device_id=peer, device_id_type=MESH,
    )


def kernel(
    grad_scale, curv_scale, code_ref, x_hbm, y_hbm, w_hbm, out,
    xg, w, y, pt, own, hold_p, hold_m, sb_p, sb_m, s2_p, s2_m, rb_p, rb_m, r2_p, r2_m,
    et, g_own, m_own, g_send, m_send, g_recv, m_recv, h_send, n_send, h_recv, n_recv,
    load_sem, xs, xr, rs_s, rs_r, ag_s, ag_r, co_s, co_r, zs, zr, fs, fr,
):
    rep, row, col = lax.axis_index("rep"), lax.axis_index("row"), lax.axis_index("col")
    plane, ypos = row // 4, row % 4
    core = rep % 2
    right, left = (col + 1) % 4, (col + 3) % 4
    to_right, to_left, to_far = {"col": right}, {"col": left}, {"col": (col + 2) % 4}
    up, down = {"row": plane * 4 + (ypos + 1) % 4}, {"row": plane * 4 + (ypos + 3) % 4}
    across = {"row": (row + 4) % 8}
    twin = {"rep": rep - core + (1 - core)}
    zmate = {"rep": (rep + 2) % 4}
    rows, cols = w.shape
    nc = cols // AVG
    half = rows // 2
    mid = cols // 2

    loads = [
        pltpu.make_async_copy(x_hbm, xg.at[:, 0:2], load_sem.at[0]),
        pltpu.make_async_copy(w_hbm, w, load_sem.at[1]),
        pltpu.make_async_copy(y_hbm, y, load_sem.at[2]),
    ]
    for load in loads:
        load.start()

    barrier = pltpu.get_barrier_semaphore()
    peers = (to_right, to_left, to_far, up, down, across, twin, zmate)
    for peer in peers:
        pl.semaphore_signal(barrier, inc=1, device_id=peer, device_id_type=MESH)
    pl.semaphore_wait(barrier, len(peers))
    loads[0].wait()

    def pass_on(slot, part, peer, landing, share=None):
        lo, hi, semaphore = (0, 4, unit(landing, part)) if share is None else (2 * share, 2 * share + 2, 16 + share)
        copy = remote(
            xg.at[lo:hi, unit(slot, part)], xg.at[lo:hi, unit(landing, part)], xs, xr.at[semaphore], peer
        )
        copy.start()

    def arrived(slot, part, share=None):
        u = unit(slot, part)
        lo, hi, semaphore = (0, 4, u) if share is None else (2 * share, 2 * share + 2, 16 + share)
        remote(xg.at[lo:hi, u], xg.at[lo:hi, u], xs, xr.at[semaphore], across).wait_recv()

    for part in range(2):
        pass_on(0, part, across, 1)
        pass_on(0, part, up, 3)
        pass_on(0, part, down, 2)

    loads[1].wait()
    loads[2].wait()

    slot_rows = []
    other = 1 - plane
    for pl_, dy in ((plane, 0), (other, 0), (plane, 1), (plane, 3), (plane, 2), (other, 1), (other, 3), (other, 2)):
        slot_rows.append(pl_ * 4 + (ypos + dy) % 4)

    def members(group):
        lo, hi = GROUPS[group]
        pieces = [xg[(col + k) % 4, lo:hi].reshape((hi - lo) * SUB, rows) for k in range(4)]
        return jnp.concatenate(pieces, axis=0)

    def put(ref, kind, group, lanes, value):
        lo, hi = GROUPS[group]
        ref[kind, lo:hi, :, lanes] = value.reshape(hi - lo, SUB, value.shape[-1])

    def get(ref, kind, group, lanes):
        lo, hi = GROUPS[group]
        value = ref[kind, lo:hi, :, lanes]
        return value.reshape((hi - lo) * SUB, value.shape[-1])

    BLOCK = 256

    def sums_of(kind, group, lanes):
        n = (GROUPS[group][1] - GROUPS[group][0]) * SUB
        if kind == TAN:
            sums = lax.dot_general(
                members(group), pt[lanes, :], (((1,), (1,)), ((), ())), preferred_element_type=F32
            )
            return [sums[k * n:(k + 1) * n] for k in range(4)]
        sums = jnp.dot(members(group), w[:, lanes], preferred_element_type=F32)
        parts = []
        for k in range(4):
            wanted = []
            for u in range(*GROUPS[group]):
                s, h = SLOTS[u]
                mine = (slot_rows[s] // 2 == col).astype(F32)
                wanted.append(y[slot_rows[s] % 2, (col + k) % 4, h, :, lanes].astype(F32) * mine)
            parts.append(sums[k * n:(k + 1) * n] - jnp.concatenate(wanted, axis=0))
        return parts

    def partial(kind, group, hold=False):
        def low(j, carry):
            lanes = pl.ds(pl.multiple_of(j * BLOCK, BLOCK), BLOCK)
            parts = sums_of(kind, group, lanes)
            put(own, kind, group, lanes, parts[0])
            put(hold_p, kind, group, lanes, parts[1])
            put(sb_p, kind, group, lanes, parts[2].astype(BF))
            put(sb_m, kind, group, lanes, parts[3].astype(BF))
            return carry

        def high(j, carry):
            lanes = pl.ds(pl.multiple_of(j * BLOCK + mid, BLOCK), BLOCK)
            parts = sums_of(kind, group, lanes)
            put(own, kind, group, lanes, parts[0])
            put(sb_p, kind, group, lanes, parts[1].astype(BF))
            put(sb_m, kind, group, lanes, parts[2].astype(BF))
            put(hold_m, kind, group, pl.ds(pl.multiple_of(j * BLOCK, BLOCK), BLOCK), parts[3])
            return carry

        lax.fori_loop(0, mid // BLOCK, low, 0)
        lax.fori_loop(0, mid // BLOCK, high, 0)
        if not hold:
            for copy in first_hop(kind, group):
                copy.start()

    def hop(kind, group, number, source, target, peer):
        lo, hi = GROUPS[group]
        return remote(
            source.at[kind, lo:hi], target.at[kind, lo:hi],
            rs_s.at[number], rs_r.at[kind, 4 * group + number], peer,
        )

    def first_hop(kind, group):
        return [hop(kind, group, 0, sb_p, rb_p, to_right), hop(kind, group, 1, sb_m, rb_m, to_left)]

    def second_hop(kind, group):
        return [hop(kind, group, 2, s2_p, r2_p, to_right), hop(kind, group, 3, s2_m, r2_m, to_left)]

    def relay(kind, group):
        low, high, every = slice(0, mid), slice(mid, cols), slice(0, mid)
        first, second = first_hop(kind, group), second_hop(kind, group)
        first[0].wait_recv()
        put(s2_p, kind, group, every, (get(hold_p, kind, group, every) + get(rb_p, kind, group, low).astype(F32)).astype(BF))
        second[0].start()
        first[1].wait_recv()
        put(s2_m, kind, group, every, (get(hold_m, kind, group, every) + get(rb_m, kind, group, high).astype(F32)).astype(BF))
        second[1].start()

    LAST = len(GROUPS) - 1

    def lane_hop(kind, out_sem, number, source, target, peer, lanes):
        lo, hi = GROUPS[LAST]
        return remote(
            source.at[kind, lo:hi, :, lanes], target.at[kind, lo:hi, :, lanes],
            rs_s.at[out_sem], rs_r.at[kind, 4 * LAST + number], peer,
        )

    PIECES = ((0, BLOCK), (BLOCK, mid), (mid, cols))

    def straight(kind, piece):
        lo, hi = PIECES[piece]
        lanes, number = slice(lo, hi), 3 * piece
        if lo < mid:
            far = lane_hop(kind, 2, number + 2, s2_p, r2_p, to_far, lanes)
        else:
            far = lane_hop(kind, 3, number + 2, s2_m, r2_m, to_far, slice(lo - mid, hi - mid))
        return [
            lane_hop(kind, 0, number, sb_p, rb_p, to_right, lanes),
            lane_hop(kind, 1, number + 1, sb_m, rb_m, to_left, lanes),
            far,
        ]

    def partial_last(kind, hold=False):
        def low(j, carry):
            lanes = pl.ds(pl.multiple_of(j * BLOCK, BLOCK), BLOCK)
            parts = sums_of(kind, LAST, lanes)
            put(own, kind, LAST, lanes, parts[0])
            put(sb_p, kind, LAST, lanes, parts[1].astype(BF))
            put(s2_p, kind, LAST, lanes, parts[2].astype(BF))
            put(sb_m, kind, LAST, lanes, parts[3].astype(BF))
            return carry

        def high(j, carry):
            lanes = pl.ds(pl.multiple_of(j * BLOCK + mid, BLOCK), BLOCK)
            parts = sums_of(kind, LAST, lanes)
            put(own, kind, LAST, lanes, parts[0])
            put(sb_p, kind, LAST, lanes, parts[1].astype(BF))
            put(s2_m, kind, LAST, pl.ds(pl.multiple_of(j * BLOCK, BLOCK), BLOCK), parts[2].astype(BF))
            put(sb_m, kind, LAST, lanes, parts[3].astype(BF))
            return carry

        for piece, (body, lo, hi) in enumerate(((low, 0, 1), (low, 1, 2), (high, 0, mid // BLOCK))):
            lax.fori_loop(lo, hi, body, 0)
            if not hold:
                for copy in straight(kind, piece):
                    copy.start()

    def reduced(kind, piece):
        lo, hi = PIECES[piece]
        if piece != 1:
            for group in range(LAST):
                second_hop(kind, group)[0 if lo < mid else 1].wait_recv()
        for copy in straight(kind, piece):
            copy.wait_recv()
        lanes, ref = slice(lo, hi), rb_p if lo < mid else rb_m
        put(own, kind, LAST, lanes, get(own, kind, LAST, lanes) + get(ref, kind, LAST, lanes).astype(F32))

    def probe_signs():
        code = code_ref[0, 0] * 1013904223
        lane = lax.broadcasted_iota(jnp.int32, (SUB, 512), 1) * 1664525
        sub = lax.broadcasted_iota(jnp.int32, (SUB, 512), 0) * 22695477
        base = lane + sub + code

        def step(j, carry):
            for i in range(rows // 512):
                mixed = base + (j * (SUB * 22695477) + wrapped(i * 512 * 1664525))
                mixed = mixed ^ mixed >> 15 & 131071
                mixed = mixed * 1274126177
                mixed = mixed ^ mixed >> 13 & 524287
                parity = mixed >> 7 & 1
                pt[pl.ds(pl.multiple_of(j * SUB, SUB), SUB), i * 512:(i + 1) * 512] = (
                    (1 - 2 * parity).astype(F32).astype(BF)
                )
            return carry

        lax.fori_loop(0, cols // SUB, step, 0)

    partial(ERR, 0)
    probe_signs()
    partial(TAN, 0)

    for s in (1, 2, 3):
        arrived(s, 0)
    pass_on(3, 0, up, 4)
    pass_on(2, 0, across, 5)
    pass_on(1, 0, up, 6)
    partial(ERR, 1)
    relay(ERR, 0)
    partial(TAN, 1)
    relay(TAN, 0)

    for s in (1, 2, 3):
        arrived(s, 1)
    pass_on(2, 1, down, 4)
    pass_on(3, 1, across, 6)
    pass_on(1, 1, down, 5)
    partial(ERR, 2)
    relay(ERR, 1)
    partial(TAN, 2)
    relay(TAN, 1)

    arrived(4, 0)
    pass_on(4, 0, across, 7)
    arrived(5, 0)
    arrived(4, 1)
    partial(ERR, 3)
    relay(ERR, 2)
    partial(TAN, 3, hold=True)
    relay(TAN, 2)

    arrived(6, 0)
    arrived(6, 1)
    pass_on(6, 1, up, 7, 0)
    arrived(5, 1)
    pass_on(5, 1, down, 7, 1)
    partial(ERR, 4)
    relay(ERR, 3)

    arrived(7, 0)
    arrived(7, 1, 0)
    arrived(7, 1, 1)
    relay(ERR, 4)
    partial_last(ERR)
    partial(TAN, 4, hold=True)
    reduced(ERR, 0)

    def own_block(kind, c):
        area = et.at[kind, c, col]
        return [
            remote(area, area, ag_s.at[0], ag_r.at[kind, 0, c], to_right),
            remote(area, area, ag_s.at[1], ag_r.at[kind, 1, c], to_left),
        ]

    def far_block(kind, c):
        first, second = slice(0, AVG // 2), slice(AVG // 2, AVG)
        low, high = et.at[kind, c, left, first], et.at[kind, c, right, second]
        return [
            remote(low, low, ag_s.at[2], ag_r.at[kind, 2, c], to_right),
            remote(high, high, ag_s.at[3], ag_r.at[kind, 3, c], to_left),
        ]

    def first_rows(part):
        return slice(part * AVG // 2, (part + 1) * AVG // 2)

    def first_block(part):
        area = et.at[ERR, 0, col, first_rows(part)]
        return [
            remote(area, area, ag_s.at[0], (fr.at[1] if part else ag_r.at[ERR, 0, 0]), to_right),
            remote(area, area, ag_s.at[1], (fr.at[2] if part else ag_r.at[ERR, 1, 0]), to_left),
            remote(area, area, ag_s.at[2 + part], ag_r.at[ERR, 2 + part, 0], to_far),
        ]

    PARTS = 2
    PART = half // PARTS

    def twin_block(c, p):
        return remote(g_send.at[c, p], g_recv.at[c, p], co_s.at[0], co_r.at[p, c], twin)

    def twin_means(c):
        return remote(m_send.at[c], m_recv.at[c], co_s.at[1], co_r.at[PARTS, c], twin)

    def z_block(c, p):
        return remote(h_send.at[c, p], h_recv.at[c, p], zs.at[0], zr.at[p, c], zmate)

    def z_means(c):
        return remote(n_send.at[c], n_recv.at[c], zs.at[1], zr.at[PARTS, c], zmate)

    def result(c, p):
        area = out.at[
            pl.ds(pl.multiple_of(core * half + p * PART, PART), PART), pl.ds(pl.multiple_of(c * AVG, AVG), AVG)
        ]
        return remote(area, area, fs, fr.at[0], twin)

    units = own.shape[1]
    tokens = units * SUB

    def share(kind, c):
        lanes = pl.ds(pl.multiple_of(c * AVG, AVG), AVG)
        within = pl.ds(pl.multiple_of(c % (nc // 2) * AVG, AVG), AVG)

        def all_of(ref, lanes):
            return ref[kind, :, :, lanes].reshape(tokens, AVG).astype(F32)

        def finish(direct, relayed):
            total = all_of(own, lanes) + all_of(direct, lanes) + all_of(relayed, within)
            et[kind, c, col] = total.T.astype(BF)

        @pl.when(c < nc // 2)
        def _():
            finish(rb_m, r2_p)

        @pl.when(c >= nc // 2)
        def _():
            finish(rb_p, r2_m)

    def send_share(kind, c):
        share(kind, c)
        for copy in own_block(kind, c):
            copy.start()

    def far_share(kind, c):
        own_copies, far_copies = own_block(kind, c), far_block(kind, c)
        for mine, theirs in zip(own_copies, far_copies):
            mine.wait_recv()
            theirs.start()

    def whole(kind, c):
        for copy in far_block(kind, c):
            copy.wait_recv()
        return jnp.concatenate([et[kind, c, k] for k in range(4)], axis=1)

    def product(block, owner, p):
        start = pl.multiple_of(owner * half + p * PART, PART)
        x = xg[:, :, :, pl.ds(start, PART)].reshape(4 * tokens, PART)
        return jnp.dot(block, x, preferred_element_type=F32), pl.ds(start, PART)

    def contract(e, *tangents):
        blocks = [] if e is None else [whole(ERR, e)]
        blocks += [whole(TAN, t) for t in tangents]
        both = jnp.concatenate(blocks, axis=0)
        before = len(blocks) - len(tangents)

        def means(sums, lanes, ref, k, p):
            signs = pl.ds(pl.multiple_of(tangents[k] * AVG, AVG), AVG)
            sums = sums[(before + k) * AVG:(before + k + 1) * AVG]
            mean = jnp.sum(sums * pt[signs, lanes].astype(F32), axis=0, keepdims=True) * curv_scale
            for j in range(PART // 128):
                at = p * (PART // 128) + j
                ref[at:at + 1, :] = mean[:, j * 128:(j + 1) * 128]

        for p in range(PARTS):
            sums, lanes = product(both, 1 - core, p)
            if e is not None:
                g_send[e, p] = (sums[:AVG] * grad_scale).astype(BF)
                twin_block(e, p).start()
            for k, t in enumerate(tangents):
                means(sums, lanes, m_send.at[t], k, p)
        for t in tangents:
            twin_means(t).start()
        for p in range(PARTS):
            sums, lanes = product(both, core, p)
            if e is not None:
                g_own[p] = sums[:AVG] * grad_scale
            for k in range(len(tangents)):
                means(sums, lanes, m_own.at[k], k, p)

    def reduce_means(*tangents):
        for k, t in enumerate(tangents):
            twin_means(t).wait_recv()
            n_send[t] = m_own[k] + m_recv[t]
            z_means(t).start()

    def reduce_twin(e):
        for p in range(PARTS):
            twin_block(e, p).wait_recv()
            h_send[e, p] = (g_own[p] + g_recv[e, p].astype(F32)).astype(BF)

    def divide(c):
        z_means(c).wait_recv()
        means = n_send[c] + n_recv[c]
        denom = jnp.maximum(jnp.abs(means), 0.25)
        columns = pl.ds(pl.multiple_of(c * AVG, AVG), AVG)
        for p in range(PARTS):
            z_block(c, p).wait_recv()
            for k in range(PART // 128):
                lanes = slice(k * 128, (k + 1) * 128)
                at = p * (PART // 128) + k
                gradient = h_send[c, p, :, lanes].astype(F32) + h_recv[c, p, :, lanes].astype(F32)
                out[pl.ds(pl.multiple_of(core * half + at * 128, 128), 128), columns] = (
                    gradient / denom[at:at + 1, :]
                ).T.astype(BF)
            result(c, p).start()

    def z_start(c):
        for p in range(PARTS):
            z_block(c, p).start()

    def first_twin(part, p):
        rows_ = first_rows(part)
        return remote(
            g_send.at[0, p, rows_], g_recv.at[0, p, rows_], co_s.at[0], (fr.at[3 + p] if part else co_r.at[p, 0]), twin
        )

    def first_z(part, p):
        rows_ = first_rows(part)
        return remote(h_send.at[0, p, rows_], h_recv.at[0, p, rows_], zs.at[0], zr.at[p, 0], zmate)

    def first_contract(part):
        for copy in first_block(part):
            copy.wait_recv()
        rows_ = first_rows(part)
        errors = jnp.concatenate([et[ERR, 0, k, rows_] for k in range(4)], axis=1)
        for p in range(PARTS):
            g_send[0, p, rows_] = (product(errors, 1 - core, p)[0] * grad_scale).astype(BF)
            first_twin(part, p).start()
        for p in range(PARTS):
            g_own[p, rows_] = product(errors, core, p)[0] * grad_scale

    def first_reduce(part):
        rows_ = first_rows(part)
        for p in range(PARTS):
            first_twin(part, p).wait_recv()
            h_send[0, p, rows_] = (g_own[p, rows_] + g_recv[0, p, rows_].astype(F32)).astype(BF)
            first_z(part, p).start()

    share(ERR, 0)
    for part in range(2):
        for copy in first_block(part):
            copy.start()
    send_share(ERR, 1)
    reduced(ERR, 1)
    send_share(ERR, 2)
    for copy in first_hop(TAN, 3):
        copy.start()
    partial_last(TAN, hold=True)
    first_contract(0)
    first_reduce(0)
    first_contract(1)
    far_share(ERR, 1)
    for copy in first_hop(TAN, 4):
        copy.start()
    first_reduce(1)
    send_share(ERR, 3)
    relay(TAN, 3)

    BACK, LAG, PAIRED = 5, 9, nc // 2

    def main(t, carry):
        @pl.when(t + 1 < nc)
        def _():
            far_share(ERR, t + 1)

        @pl.when((t >= BACK - 1) & (t < BACK - 1 + PAIRED))
        def _():
            far_share(TAN, t - (BACK - 1))

        @pl.when((t == PAIRED + 4) | (t == PAIRED + 5))
        def _():
            first = PAIRED + 2 * (t - PAIRED - 4)
            far_share(TAN, first)
            far_share(TAN, first + 1)

        @pl.when(t == 1)
        def _():
            for piece in range(len(PIECES)):
                for copy in straight(TAN, piece):
                    copy.start()
            reduced(ERR, 2)

        @pl.when(t + 3 < nc)
        def _():
            send_share(ERR, t + 3)

        @pl.when((t >= 3) & (t < PAIRED + 2))
        def _():
            send_share(TAN, t - 2)

        @pl.when((t == PAIRED + 2) | (t == PAIRED + 3))
        def _():
            first = PAIRED + 2 * (t - PAIRED - 2)
            send_share(TAN, first)
            send_share(TAN, first + 1)

        @pl.when(t < BACK)
        def _():
            contract(t)

        @pl.when((t >= BACK) & (t < nc))
        def _():
            contract(t, t - BACK)
            reduce_means(t - BACK)

        @pl.when(t == nc)
        def _():
            contract(None, nc - BACK)
            reduce_means(nc - BACK)

        @pl.when((t == nc + 1) | (t == nc + 2))
        def _():
            first = PAIRED + 2 * (t - nc - 1)
            contract(None, first, first + 1)
            reduce_means(first, first + 1)

        @pl.when(t < nc)
        def _():
            reduce_twin(t)

        @pl.when(t < 6)
        def _():
            z_start(t)

        @pl.when((t == 7) | (t == 9))
        def _():
            z_start((t + 5) // 2)

        @pl.when(t == 1)
        def _():
            relay(TAN, 4)

        @pl.when(t == 2)
        def _():
            for piece in range(len(PIECES)):
                reduced(TAN, piece)
            send_share(TAN, 0)

        @pl.when(t >= LAG)
        def _():
            divide(t - LAG)

        return carry

    lax.fori_loop(1, nc + LAG, main, 0)

    def left_for_good(area, semaphore):
        remote(area, area, semaphore, fr.at[0], twin).wait_send()

    left_for_good(xg.at[:, 0:14], xs)
    for k, ref in enumerate((sb_p, sb_m, s2_p, s2_m)):
        left_for_good(ref, rs_s.at[k])
    for k in range(2):
        left_for_good(et.at[:, :, 0], ag_s.at[k])
        left_for_good(et.at[:, :, 0, 0:AVG // 2], ag_s.at[2 + k])
    for k, (block, means) in enumerate(((g_send, m_send), (h_send, n_send))):
        left_for_good(block, (co_s, zs)[k].at[0])
        left_for_good(means, (co_s, zs)[k].at[1])
    area = out.at[0:half]
    remote(area, area, fs, fr.at[0], twin).wait()


def write_out(step, out, sems):
    n = sems.shape[0]
    size = step.shape[0] // n
    copies = [
        pltpu.make_async_copy(step.at[pl.ds(k * size, size)], out.at[pl.ds(k * size, size)], sems.at[k])
        for k in range(n)
    ]
    for copy in copies:
        copy.start()
    for copy in copies:
        copy.wait()


def shards(activations, target, weight, probe_codes):
    share, rows = activations.shape
    cols = weight.shape[1]
    nc = cols // AVG
    tokens_micro = share * lax.axis_size("row")
    total = tokens_micro * lax.axis_size("rep")
    x = activations.reshape(4, 2, SUB, rows)
    y = target.reshape(2, 4, 2, SUB, cols)
    half = rows // 2
    vmem = pltpu.VMEM
    dma = pltpu.SemaphoreType.DMA
    step = pl.pallas_call(
        functools.partial(kernel, 1.0 / math.sqrt(total), 1.0 / total / AVG),
        out_shape=pltpu.VMEM((rows, cols), BF),
        in_specs=[pl.BlockSpec(memory_space=pltpu.SMEM)] + [pl.BlockSpec(memory_space=pltpu.MemorySpace.HBM)] * 3,
        out_specs=pl.BlockSpec(memory_space=pltpu.VMEM),
        scratch_shapes=[
            vmem((4, 16, SUB, rows), BF),
            vmem((rows, cols), BF),
            vmem((2, 4, 2, SUB, cols), BF),
            vmem((cols, rows), BF),
            vmem((2, 16, SUB, cols), F32),
            vmem((2, 16, SUB, cols // 2), F32),
            vmem((2, 16, SUB, cols // 2), F32),
            vmem((2, 16, SUB, cols), BF),
            vmem((2, 16, SUB, cols), BF),
            vmem((2, 16, SUB, cols // 2), BF),
            vmem((2, 16, SUB, cols // 2), BF),
            vmem((2, 16, SUB, cols), BF),
            vmem((2, 16, SUB, cols), BF),
            vmem((2, 16, SUB, cols // 2), BF),
            vmem((2, 16, SUB, cols // 2), BF),
            vmem((2, nc, 4, AVG, 256), BF),
            vmem((2, AVG, half // 2), F32),
            vmem((2, 8, 128), F32),
            vmem((nc, 2, AVG, half // 2), BF),
            vmem((nc, 8, 128), F32),
            vmem((nc, 2, AVG, half // 2), BF),
            vmem((nc, 8, 128), F32),
            vmem((nc, 2, AVG, half // 2), BF),
            vmem((nc, 8, 128), F32),
            vmem((nc, 2, AVG, half // 2), BF),
            vmem((nc, 8, 128), F32),
            dma((3,)),
            dma(()),
            dma((18,)),
            dma((4,)),
            dma((2, 29)),
            dma((4,)),
            dma((2, 4, nc)),
            dma((2,)),
            dma((3, nc)),
            dma((2,)),
            dma((3, nc)),
            dma(()),
            dma((5,)),
        ],
        compiler_params=pltpu.CompilerParams(
            collective_id=0, has_side_effects=True, vmem_limit_bytes=50 * 1024 * 1024
        ),
    )(probe_codes, *(pltpu.with_memory_space_constraint(v, pltpu.MemorySpace.HBM) for v in (x, y, weight)))
    return pl.pallas_call(
        write_out,
        out_shape=jax.ShapeDtypeStruct((rows, cols), BF),
        in_specs=[pl.BlockSpec(memory_space=pltpu.VMEM)],
        out_specs=pl.BlockSpec(memory_space=pltpu.MemorySpace.HBM),
        scratch_shapes=[dma((4,))],
        compiler_params=pltpu.CompilerParams(vmem_limit_bytes=1024 * 1024),
    )(step)


def solution(mesh):
    placed = (P(("rep", "row"), "col"), P(("rep", "col"), "row"), P("col", "row"), P("col", "row"))
    return jax.shard_map(
        shards, mesh=mesh, in_specs=placed, out_specs=P("col", "row"), check_vma=False
    )
```
